32 devices in a mesh: groups: 2 (over x), dp: 16 (over z, y, core).
Axes of the slice: x: 2, y: 2, z: 4, core: 2. Of those that a mesh axis runs over, the one named last changes fastest.
Arguments:
- tokens: bfloat16 [24576, 1024], P(('groups', 'dp')), parts along dimension 0, may hold values from -6 to 6
- token_mask: int32 [32, 768], P(('groups', 'dp')), parts along dimension 0, may hold values 0 or 1
- span_ids: int32 [32, 768], P(('groups', 'dp')), parts along dimension 0, may hold values from 0 to 191, never falling along the last dimension, each value on 1 to 8 neighbouring positions
- norm_gain: float32 [1024], replicated, may hold values from 0.1 to 1.9
- norm_shift: float32 [1024], replicated, may hold values from -3 to 3
- w_up: bfloat16 [1024, 4096], P(None, 'dp'), may hold values from -0.1875 to 0.1875
- b_up: float32 [4096], replicated, may hold values from -3 to 3
- w_down: bfloat16 [4096, 1024], P(None, 'dp'), may hold values from -0.09375 to 0.09375
Outputs:
- whitened: float32 [6144, 1024], P(('groups', 'dp')), parts along dimension 0
The draws below stay inside these ranges and needn't reach their ends.
There are 2 independent parts, one for each index of `groups`. The reference program is written for one: setup_inputs(seed, part) draws one part's arguments, and reference() takes and returns one part's arrays. A program takes and returns all parts, laid end to end along the dimension named above; an argument that names none is the same for every part. Nothing has to cross between parts.
Inputs may be any that keep to these rules, and one draw needn't show every extreme that they name: `span_ids`: in each row the span numbers never fall, every span 0 to 191 holds 1 to 8 tokens, and one holds exactly 8.
All inputs are finite; a program needn't handle non-finite values. No bound on the sum of `token_mask` on one device may be relied on, other than what follows from the above.
Results may differ from the reference program's by a relative error of at most 0.0095.
Values may be sent and summed in bfloat16 or wider, within the bound.
A program may use at most 128 MiB of HBM per device.

```python
import math
import jax
import jax.numpy as jnp
import numpy as np
from jax import lax

D = 1024
FF = 4096
TOK_DEV = 768
MOST = 8
SEG_DEV = 192
TOKENS = 12288
ROWS = 3072
N_DP = 16


def with_ends(entries, key, least, largest):
    extent = entries.shape
    spot = [jax.random.randint(jax.random.fold_in(key, axis), (), 0, extent[axis]) for axis in range(len(extent))]
    entries = entries.at[tuple(spot)].set(least)
    longest = extent.index(max(extent))
    spot[longest] = (spot[longest] + 1) % extent[longest]
    return entries.at[tuple(spot)].set(largest)


def shard_levels(key, shape, split, least, high):
    level = 1.0
    for position, blocks in split:
        draws = jax.random.uniform(jax.random.fold_in(jax.random.fold_in(key, 6), position), (blocks,), jnp.float32, least / len(split), high / len(split))
        level = level * jnp.repeat(jnp.exp(draws), shape[position] // blocks).reshape((-1,) + (1,) * (len(shape) - 1 - position))
    return level


def profile(amount, total, reach, lean):
    weights = [(1 << 20) // math.isqrt(standing ** lean) + 1 for standing in range(2, amount + 1)]
    spare, holding = total - reach - (amount - 1), [1] * (amount - 1)
    while spare > 0:
        free = [i for i in range(amount - 1) if holding[i] < reach]
        mass, left = sum([weights[i] for i in free]), spare
        for i in free:
            extra = min(reach - holding[i], max(1, left * weights[i] // mass), spare)
            holding[i] = holding[i] + extra
            spare = spare - extra
    return np.array([reach] + holding)


def uneven_parts(rng, count, total, reach, lean):
    if count == 2:
        one = jax.random.randint(rng, (), max(1, total - reach), min(reach, total - 1) + 1)
        return jnp.stack([one, total - one])
    sizes = jnp.asarray(profile(count, total, reach, lean), jnp.int32)
    pairs = (count - 1) // 2
    giver, receiver = sizes[1:1 + 2 * pairs:2], sizes[2:2 + 2 * pairs:2]
    margin = jnp.minimum(giver - 1, reach - receiver)
    shifted = jax.random.randint(jax.random.fold_in(rng, 1), (pairs,), 0, 1 << 20) % (margin + 1)
    sizes = sizes.at[1:1 + 2 * pairs:2].set(giver - shifted).at[2:2 + 2 * pairs:2].set(receiver + shifted)
    return sizes[jax.random.permutation(jax.random.fold_in(rng, 2), count)]


def normal_values(stream_key, shape, scale, limit, split=(), kind=jnp.bfloat16):
    factor_of = shard_levels(stream_key, shape, split, -0.22, 0.18) if split else 1.0
    drawn = jax.random.normal(stream_key, shape, jnp.float32) * scale * factor_of
    return jnp.minimum(jnp.maximum(drawn, -limit), limit).astype(kind)


def setup_inputs(seed: int = 0, part: int = 0) -> dict:
    keys = jax.random.split(jax.random.key(seed), 9)
    own_keys = jax.random.split(jax.random.fold_in(keys[8], part), 9)
    return {
        "tokens": normal_values(own_keys[0], (TOKENS, D), 1.0, 6.0, ((0, 16),)),
        "token_mask": with_ends((jax.random.randint(own_keys[1], (N_DP, TOK_DEV), 0, 8) < 7).astype(jnp.int32), jax.random.fold_in(own_keys[1], 1), 0, 1),
        "span_ids": jax.vmap(lambda own: jnp.searchsorted(jnp.cumsum(uneven_parts(own, SEG_DEV, TOK_DEV, MOST, 0)), jnp.arange(TOK_DEV), side="right"))(jax.random.split(own_keys[2], N_DP)).reshape((N_DP, TOK_DEV)).astype(jnp.int32),
        "norm_gain": jnp.clip(1.0 + 0.18 * jax.random.normal(keys[3], (D,), jnp.float32), 0.1, 1.9),
        "norm_shift": normal_values(keys[4], (D,), 0.5, 3.0, (), jnp.float32),
        "w_up": normal_values(keys[5], (D, FF), D ** -0.5, 0.1875, ((1, 16),)),
        "b_up": normal_values(keys[6], (FF,), 0.5, 3.0, (), jnp.float32),
        "w_down": normal_values(keys[7], (FF, D), FF ** -0.5, 0.09375, ((1, 16),)),
    }


def shard_pass(tokens_shard, mask_row, span_row, norm_gain, norm_shift, w_up, b_up, w_down):
    values = tokens_shard.astype(jnp.float32)
    center = lax.optimization_barrier(jnp.mean(values, axis=1, keepdims=True))
    spread = lax.optimization_barrier(jnp.mean((values - center) ** 2, axis=1, keepdims=True))
    normed = ((values - center) * lax.rsqrt(spread + 1e-05) * norm_gain + norm_shift).astype(jnp.bfloat16)
    before = jnp.dot(normed.astype(jnp.float32), w_up.astype(jnp.float32), preferred_element_type=jnp.float32) + b_up
    hidden = jax.nn.gelu(before, approximate=False).astype(jnp.bfloat16)
    block_out = (values + jnp.dot(hidden.astype(jnp.float32), w_down.astype(jnp.float32), preferred_element_type=jnp.float32)).astype(jnp.bfloat16)
    labels = jnp.arange(SEG_DEV, dtype=jnp.int32)[:, None]
    select = (span_row[None, :] == labels) & (mask_row[None, :] == 1)
    sums = jnp.dot(select.astype(jnp.bfloat16).astype(jnp.float32), block_out.astype(jnp.float32), preferred_element_type=jnp.float32)
    counts = lax.optimization_barrier(jnp.sum(select.astype(jnp.float32), axis=1))
    return (sums / jnp.maximum(counts, 1.0)[:, None]).astype(jnp.bfloat16)

def reference(tokens, token_mask, span_ids, norm_gain, norm_shift, w_up, b_up, w_down):
    shards = tokens.reshape(N_DP, TOK_DEV, D)

    def one_shard(items):
        return shard_pass(items[0], items[1], items[2], norm_gain, norm_shift, w_up, b_up, w_down)
    pooled = lax.map(one_shard, (shards, token_mask, span_ids)).reshape(ROWS, D)
    gram = jnp.dot(pooled.T.astype(jnp.float32), pooled.astype(jnp.float32), preferred_element_type=jnp.float32)
    lower = jnp.linalg.cholesky(gram)
    solved = jax.scipy.linalg.solve_triangular(lower, pooled.astype(jnp.float32).T, lower=True)
    return math.sqrt(ROWS) * solved.T
```

```python
import functools
import math

import jax
import jax.numpy as jnp
from jax import lax
from jax.experimental import pallas as pl
from jax.experimental.pallas import tpu as pltpu
from jax.sharding import PartitionSpec as P

SEG_DEV = 192
BLOCK = 128
HIGHEST = lax.Precision.HIGHEST


def inverse_factor(src, dst):
    lane = lax.broadcasted_iota(jnp.int32, (8, BLOCK), 1)
    sub = lax.broadcasted_iota(jnp.int32, (8, BLOCK), 0)
    groups = BLOCK // 8
    held = [src[8 * q : 8 * q + 8, :BLOCK] for q in range(groups)]

    def column(block, c):
        return jnp.broadcast_to(block[:, c : c + 1], (8, BLOCK))

    def row(block, r):
        return jnp.broadcast_to(block[r : r + 1, :], (8, BLOCK))

    for p in range(groups):
        at = 8 * p
        inside = (lane >= at) & (lane < at + 8)
        raw = held[p]
        cols = [column(raw, at + c) for c in range(8)]
        work = jnp.where(inside, jnp.where(lane - at == sub, 1.0, 0.0), raw)
        done = jnp.zeros((8, BLOCK), jnp.float32)
        for j in range(8):
            here = sub == j
            pivot = row(cols[j], j)
            inv = 1.0 / pivot
            done = jnp.where(here, work * lax.rsqrt(pivot), done)
            scaled = row(work, j) * inv
            work = jnp.where(here, scaled, work - cols[j] * scaled)
            for c in range(j + 1, 8):
                scaled = row(cols[c], j) * inv
                cols[c] = jnp.where(here, scaled, cols[c] - cols[j] * scaled)
        dst[at : at + 8, :] = jnp.where(lane <= at + sub, done, 0.0)
        rows = [row(work, c) for c in range(8)]
        for q in range(p + 1, groups):
            total = jnp.where(inside, 0.0, held[q])
            for c in range(8):
                total = total - column(held[q], at + c) * rows[c]
            held[q] = total


def whiten_kernel(scale, gram_ref, rows_ref, out_ref, a, panel, inv):
    n = gram_ref.shape[0]
    extra = rows_ref.shape[1]
    a[:, :n] = gram_ref[...]
    a[:, n:] = jnp.zeros((n, a.shape[1] - n), jnp.float32)
    a[:, n : n + extra] = rows_ref[...]
    blocks = n // BLOCK

    def step(k, carry):
        lo = pl.multiple_of(k * BLOCK, BLOCK)
        panel[:, :BLOCK] = a[pl.ds(lo, BLOCK), pl.ds(lo, BLOCK)]
        inverse_factor(panel, inv)
        panel[...] = jnp.dot(
            inv[...], a[pl.ds(lo, BLOCK), :], preferred_element_type=jnp.float32, precision=HIGHEST
        )
        out_ref[pl.ds(lo, BLOCK), :] = panel[:, n : n + extra] * scale

        def trail(i, carry):
            hi = pl.multiple_of(i * BLOCK, BLOCK)
            left = panel[:, pl.ds(hi, BLOCK)].T
            a[pl.ds(hi, BLOCK), :] -= jnp.dot(
                left, panel[...], preferred_element_type=jnp.float32, precision=HIGHEST
            )
            return carry

        return lax.fori_loop(k + 1, blocks, trail, carry)

    lax.fori_loop(0, blocks, step, 0)


def whiten(gram, rows_t, scale):
    n, extra = rows_t.shape
    wide = n + (extra + BLOCK - 1) // BLOCK * BLOCK
    return pl.pallas_call(
        functools.partial(whiten_kernel, scale),
        out_shape=jax.ShapeDtypeStruct((n, extra), jnp.float32),
        in_specs=[pl.BlockSpec(memory_space=pltpu.VMEM)] * 2,
        out_specs=pl.BlockSpec(memory_space=pltpu.VMEM),
        scratch_shapes=[
            pltpu.VMEM((n, wide), jnp.float32),
            pltpu.VMEM((BLOCK, wide), jnp.float32),
            pltpu.VMEM((BLOCK, BLOCK), jnp.float32),
        ],
        compiler_params=pltpu.CompilerParams(vmem_limit_bytes=32 << 20),
    )(gram, rows_t)


def on_device(tokens, token_mask, span_ids, norm_gain, norm_shift, w_up, b_up, w_down):
    values = tokens.astype(jnp.float32)
    center = jnp.mean(values, axis=1, keepdims=True)
    spread = jnp.mean((values - center) ** 2, axis=1, keepdims=True)
    normed = ((values - center) * lax.rsqrt(spread + 1e-05) * norm_gain + norm_shift).astype(
        jnp.bfloat16
    )
    up_full, down_full = (
        lax.all_gather(w_up, "dp", axis=1, tiled=True),
        lax.all_gather(w_down, "dp", axis=1, tiled=True),
    )
    before = jnp.dot(normed, up_full, preferred_element_type=jnp.float32) + b_up
    hidden = jax.nn.gelu(before, approximate=False).astype(jnp.bfloat16)
    projected = jnp.dot(hidden, down_full, preferred_element_type=jnp.float32)
    block_out = (values + projected).astype(jnp.bfloat16)
    labels = jnp.arange(SEG_DEV, dtype=jnp.int32)[:, None]
    select = (span_ids[0][None, :] == labels) & (token_mask[0][None, :] == 1)
    sums = jnp.dot(select.astype(jnp.bfloat16), block_out, preferred_element_type=jnp.float32)
    counts = jnp.sum(select.astype(jnp.float32), axis=1)
    pooled = (sums / jnp.maximum(counts, 1.0)[:, None]).astype(jnp.bfloat16)
    every = lax.all_gather(pooled, "dp", axis=0, tiled=True)
    gram = lax.dot_general(
        every, every, (((0,), (0,)), ((), ())), preferred_element_type=jnp.float32
    )
    total_rows = SEG_DEV * lax.axis_size("dp")
    return whiten(gram, pooled.astype(jnp.float32).T, math.sqrt(total_rows)).T


def solution(mesh):
    in_specs = (
        P(("groups", "dp"), None),
        P(("groups", "dp"), None),
        P(("groups", "dp"), None),
        P(),
        P(),
        P(None, "dp"),
        P(),
        P(None, "dp"),
    )
    out_specs = P(("groups", "dp"), None)
    return jax.shard_map(
        on_device, mesh=mesh, in_specs=in_specs, out_specs=out_specs, check_vma=False
    )
```

```python
import functools
import math

import jax
import jax.numpy as jnp
from jax import lax
from jax.experimental import pallas as pl
from jax.experimental.pallas import tpu as pltpu
from jax.sharding import PartitionSpec as P

SEG_DEV = 192
BLOCK = 128
HIGHEST = lax.Precision.HIGHEST


def inverse_factor(src, dst):
    lane = lax.broadcasted_iota(jnp.int32, (8, BLOCK), 1)
    sub = lax.broadcasted_iota(jnp.int32, (8, BLOCK), 0)
    groups = BLOCK // 8
    held = [src[8 * q : 8 * q + 8, :BLOCK] for q in range(groups)]

    def column(block, c):
        return jnp.broadcast_to(block[:, c : c + 1], (8, BLOCK))

    def row(block, r):
        return jnp.broadcast_to(block[r : r + 1, :], (8, BLOCK))

    for p in range(groups):
        at = 8 * p
        inside = (lane >= at) & (lane < at + 8)
        raw = held[p]
        cols = [column(raw, at + c) for c in range(8)]
        work = jnp.where(inside, jnp.where(lane - at == sub, 1.0, 0.0), raw)
        done = jnp.zeros((8, BLOCK), jnp.float32)
        for j in range(8):
            here = sub == j
            pivot = row(cols[j], j)
            inv = 1.0 / pivot
            done = jnp.where(here, work * lax.rsqrt(pivot), done)
            scaled = row(work, j) * inv
            work = jnp.where(here, scaled, work - cols[j] * scaled)
            for c in range(j + 1, 8):
                scaled = row(cols[c], j) * inv
                cols[c] = jnp.where(here, scaled, cols[c] - cols[j] * scaled)
        dst[at : at + 8, :] = jnp.where(lane <= at + sub, done, 0.0)
        rows = [row(work, c) for c in range(8)]
        for q in range(p + 1, groups):
            total = jnp.where(inside, 0.0, held[q])
            for c in range(8):
                total = total - column(held[q], at + c) * rows[c]
            held[q] = total


def whiten_kernel(scale, gram_ref, rows_ref, out_ref, a, panel, inv):
    n = gram_ref.shape[0]
    extra = rows_ref.shape[1]
    a[:, :n] = gram_ref[...]
    a[:, n:] = jnp.zeros((n, a.shape[1] - n), jnp.float32)
    a[:, n : n + extra] = rows_ref[...]
    blocks = n // BLOCK

    def step(k, carry):
        lo = pl.multiple_of(k * BLOCK, BLOCK)
        panel[:, :BLOCK] = a[pl.ds(lo, BLOCK), pl.ds(lo, BLOCK)]
        inverse_factor(panel, inv)
        panel[...] = jnp.dot(
            inv[...], a[pl.ds(lo, BLOCK), :], preferred_element_type=jnp.float32, precision=HIGHEST
        )
        out_ref[pl.ds(lo, BLOCK), :] = panel[:, n : n + extra] * scale

        def trail(i, carry):
            hi = pl.multiple_of(i * BLOCK, BLOCK)
            left = panel[:, pl.ds(hi, BLOCK)].T
            a[pl.ds(hi, BLOCK), :] -= jnp.dot(
                left, panel[...], preferred_element_type=jnp.float32, precision=HIGHEST
            )
            return carry

        return lax.fori_loop(k + 1, blocks, trail, carry)

    lax.fori_loop(0, blocks, step, 0)


def whiten(gram, rows_t, scale):
    n, extra = rows_t.shape
    wide = n + (extra + BLOCK - 1) // BLOCK * BLOCK
    return pl.pallas_call(
        functools.partial(whiten_kernel, scale),
        out_shape=jax.ShapeDtypeStruct((n, extra), jnp.float32),
        in_specs=[pl.BlockSpec(memory_space=pltpu.VMEM)] * 2,
        out_specs=pl.BlockSpec(memory_space=pltpu.VMEM),
        scratch_shapes=[
            pltpu.VMEM((n, wide), jnp.float32),
            pltpu.VMEM((BLOCK, wide), jnp.float32),
            pltpu.VMEM((BLOCK, BLOCK), jnp.float32),
        ],
        compiler_params=pltpu.CompilerParams(vmem_limit_bytes=32 << 20),
    )(gram, rows_t)


def ring_kernel(chips, count, *refs):
    ins, outs = refs[:count], refs[count : 2 * count]
    ring_send, ring_recv, core_send, core_recv, own_sem = refs[2 * count :]
    me = lax.axis_index("dp")
    core, chip = lax.rem(me, 2), me // 2
    half = chips // 2
    odd = lax.rem(chip, 2)
    place = (1 - odd) * (chip // 2) + odd * (chips - 1 - chip // 2)
    turn = 1 - 2 * core
    partner = me + turn

    def device(q):
        q = lax.rem(q + 2 * chips, chips)
        back = q // half
        return 2 * ((1 - back) * 2 * q + back * (2 * (chips - 1 - q) + 1)) + core

    ahead, behind = device(place + turn), device(place - turn)
    barrier = pltpu.get_barrier_semaphore()
    for other in (ahead, behind, partner):
        pl.semaphore_signal(
            barrier, inc=1, device_id={"dp": other}, device_id_type=pl.DeviceIdType.MESH
        )
    pl.semaphore_wait(barrier, 3)

    steps = (half, chips - 1 - half)
    started, across = [], []

    def send(a, source, slot, way, step):
        copy = pltpu.make_async_remote_copy(
            src_ref=source,
            dst_ref=outs[a].at[slot],
            send_sem=ring_send.at[a, way, step],
            recv_sem=ring_recv.at[a, way, step],
            device_id={"dp": (ahead, behind)[way]},
            device_id_type=pl.DeviceIdType.MESH,
        )
        copy.start()
        started.append(copy)
        return copy

    def share(a, source, slot, index):
        copy = pltpu.make_async_remote_copy(
            src_ref=source,
            dst_ref=outs[a].at[slot],
            send_sem=core_send.at[a, index],
            recv_sem=core_recv.at[a, index],
            device_id={"dp": partner},
            device_id_type=pl.DeviceIdType.MESH,
        )
        copy.start()
        across.append(copy)

    flying, local = {}, []
    for a in range(count):
        for way in range(2):
            flying[a, way] = send(a, ins[a], me, way, 0)
        share(a, ins[a], me, 0)
        local.append(pltpu.make_async_copy(ins[a], outs[a].at[me], own_sem.at[a]))
        local[-1].start()
    for step in range(half):
        for a in range(count):
            for way in range(2):
                if step >= steps[way]:
                    continue
                flying[a, way].wait_recv()
                slot = device(place - (1 + step) * turn * (1 - 2 * way))
                block = outs[a].at[slot]
                if step + 1 < steps[way]:
                    flying[a, way] = send(a, block, slot, way, step + 1)
                share(a, block, slot, 1 + way * half + step)
    for copy in local:
        copy.wait()
    for copy in started:
        copy.wait_send()
    for copy in across:
        copy.wait()


def ring_gather(blocks, collective_id):
    devices = lax.axis_size("dp")
    chips, count = devices // 2, len(blocks)
    dma = pltpu.SemaphoreType.DMA
    return pl.pallas_call(
        functools.partial(ring_kernel, chips, count),
        out_shape=[jax.ShapeDtypeStruct((devices,) + b.shape, b.dtype) for b in blocks],
        in_specs=[pl.BlockSpec(memory_space=pl.ANY)] * count,
        out_specs=[pl.BlockSpec(memory_space=pl.ANY)] * count,
        scratch_shapes=[
            dma((count, 2, chips // 2)),
            dma((count, 2, chips // 2)),
            dma((count, chips)),
            dma((count, chips)),
            dma((count,)),
        ],
        compiler_params=pltpu.CompilerParams(collective_id=collective_id, has_side_effects=True),
    )(*blocks)


def on_device(tokens, token_mask, span_ids, norm_gain, norm_shift, w_up, b_up, w_down):
    values = tokens.astype(jnp.float32)
    center = jnp.mean(values, axis=1, keepdims=True)
    spread = jnp.mean((values - center) ** 2, axis=1, keepdims=True)
    normed = ((values - center) * lax.rsqrt(spread + 1e-05) * norm_gain + norm_shift).astype(
        jnp.bfloat16
    )
    up_full, down_full = ring_gather((w_up.T, w_down.T), 0)
    width, hidden_size = tokens.shape[1], b_up.shape[0]
    up_full, down_full = up_full.reshape(hidden_size, width), down_full.reshape(width, hidden_size)
    over_last = (((1,), (1,)), ((), ()))
    before = (
        lax.dot_general(normed, up_full, over_last, preferred_element_type=jnp.float32) + b_up
    )
    hidden = jax.nn.gelu(before, approximate=False).astype(jnp.bfloat16)
    projected = lax.dot_general(
        hidden, down_full, over_last, preferred_element_type=jnp.float32
    )
    block_out = (values + projected).astype(jnp.bfloat16)
    labels = jnp.arange(SEG_DEV, dtype=jnp.int32)[:, None]
    select = (span_ids[0][None, :] == labels) & (token_mask[0][None, :] == 1)
    sums = jnp.dot(select.astype(jnp.bfloat16), block_out, preferred_element_type=jnp.float32)
    counts = jnp.sum(select.astype(jnp.float32), axis=1)
    pooled = (sums / jnp.maximum(counts, 1.0)[:, None]).astype(jnp.bfloat16)
    (every,) = ring_gather((pooled,), 1)
    every = every.reshape(-1, width)
    gram = lax.dot_general(
        every, every, (((0,), (0,)), ((), ())), preferred_element_type=jnp.float32
    )
    total_rows = SEG_DEV * lax.axis_size("dp")
    return whiten(gram, pooled.astype(jnp.float32).T, math.sqrt(total_rows)).T


def solution(mesh):
    in_specs = (
        P(("groups", "dp"), None),
        P(("groups", "dp"), None),
        P(("groups", "dp"), None),
        P(),
        P(),
        P(None, "dp"),
        P(),
        P(None, "dp"),
    )
    out_specs = P(("groups", "dp"), None)
    return jax.shard_map(
        on_device, mesh=mesh, in_specs=in_specs, out_specs=out_specs, check_vma=False
    )
```

```python
import functools
import math

import jax
import jax.numpy as jnp
from jax import lax
from jax.experimental import pallas as pl
from jax.experimental.pallas import tpu as pltpu
from jax.sharding import PartitionSpec as P

SEG_DEV = 192
BLOCK = 128
HIGHEST = lax.Precision.HIGHEST


def inverse_factor(src, dst):
    lane = lax.broadcasted_iota(jnp.int32, (8, BLOCK), 1)
    sub = lax.broadcasted_iota(jnp.int32, (8, BLOCK), 0)
    groups = BLOCK // 8
    held = [src[8 * q : 8 * q + 8, :BLOCK] for q in range(groups)]

    def column(block, c):
        return jnp.broadcast_to(block[:, c : c + 1], (8, BLOCK))

    def row(block, r):
        return jnp.broadcast_to(block[r : r + 1, :], (8, BLOCK))

    for p in range(groups):
        at = 8 * p
        inside = (lane >= at) & (lane < at + 8)
        raw = held[p]
        cols = [column(raw, at + c) for c in range(8)]
        work = jnp.where(inside, jnp.where(lane - at == sub, 1.0, 0.0), raw)
        done = jnp.zeros((8, BLOCK), jnp.float32)
        for j in range(8):
            here = sub == j
            pivot = row(cols[j], j)
            inv = 1.0 / pivot
            done = jnp.where(here, work * lax.rsqrt(pivot), done)
            scaled = row(work, j) * inv
            work = jnp.where(here, scaled, work - cols[j] * scaled)
            for c in range(j + 1, 8):
                scaled = row(cols[c], j) * inv
                cols[c] = jnp.where(here, scaled, cols[c] - cols[j] * scaled)
        dst[at : at + 8, :] = jnp.where(lane <= at + sub, done, 0.0)
        rows = [row(work, c) for c in range(8)]
        for q in range(p + 1, groups):
            total = jnp.where(inside, 0.0, held[q])
            for c in range(8):
                total = total - column(held[q], at + c) * rows[c]
            held[q] = total


def whiten_kernel(scale, gram_ref, rows_ref, out_ref, a, panel, inv):
    n = gram_ref.shape[0]
    extra = rows_ref.shape[1]
    a[:, :n] = gram_ref[...]
    a[:, n:] = jnp.zeros((n, a.shape[1] - n), jnp.float32)
    a[:, n : n + extra] = rows_ref[...]
    blocks = n // BLOCK

    def step(k, carry):
        lo = pl.multiple_of(k * BLOCK, BLOCK)
        panel[:, :BLOCK] = a[pl.ds(lo, BLOCK), pl.ds(lo, BLOCK)]
        inverse_factor(panel, inv)
        panel[...] = jnp.dot(
            inv[...], a[pl.ds(lo, BLOCK), :], preferred_element_type=jnp.float32, precision=HIGHEST
        )
        out_ref[pl.ds(lo, BLOCK), :] = panel[:, n : n + extra] * scale

        def trail(i, carry):
            hi = pl.multiple_of(i * BLOCK, BLOCK)
            left = panel[:, pl.ds(hi, BLOCK)].T
            a[pl.ds(hi, BLOCK), :] -= jnp.dot(
                left, panel[...], preferred_element_type=jnp.float32, precision=HIGHEST
            )
            return carry

        return lax.fori_loop(k + 1, blocks, trail, carry)

    lax.fori_loop(0, blocks, step, 0)


def whiten(gram, rows_t, scale):
    n, extra = rows_t.shape
    wide = n + (extra + BLOCK - 1) // BLOCK * BLOCK
    return pl.pallas_call(
        functools.partial(whiten_kernel, scale),
        out_shape=jax.ShapeDtypeStruct((n, extra), jnp.float32),
        in_specs=[pl.BlockSpec(memory_space=pltpu.VMEM)] * 2,
        out_specs=pl.BlockSpec(memory_space=pltpu.VMEM),
        scratch_shapes=[
            pltpu.VMEM((n, wide), jnp.float32),
            pltpu.VMEM((BLOCK, wide), jnp.float32),
            pltpu.VMEM((BLOCK, BLOCK), jnp.float32),
        ],
        compiler_params=pltpu.CompilerParams(vmem_limit_bytes=32 << 20),
    )(gram, rows_t)


def ring_kernel(chips, count, fused, *refs):
    if fused:
        normed, bias, up, down, hidden, down_out, up_out = refs[:7]
        ins, outs, refs = (up, down), (up_out, down_out), refs[7:]
    else:
        ins, outs, refs = refs[:count], refs[count : 2 * count], refs[2 * count :]
    ring_send, ring_recv, core_send, core_recv, own_sem = refs
    me = lax.axis_index("dp")
    core, chip = lax.rem(me, 2), me // 2
    half = chips // 2
    odd = lax.rem(chip, 2)
    place = (1 - odd) * (chip // 2) + odd * (chips - 1 - chip // 2)
    turn = 1 - 2 * core
    partner = me + turn

    def device(q):
        q = lax.rem(q + 2 * chips, chips)
        back = q // half
        return 2 * ((1 - back) * 2 * q + back * (2 * (chips - 1 - q) + 1)) + core

    ahead, behind = device(place + turn), device(place - turn)
    barrier = pltpu.get_barrier_semaphore()
    for other in (ahead, behind, partner):
        pl.semaphore_signal(
            barrier, inc=1, device_id={"dp": other}, device_id_type=pl.DeviceIdType.MESH
        )
    pl.semaphore_wait(barrier, 3)

    steps = (half, chips - 1 - half)
    started, across = [], []

    def send(a, source, slot, way, step):
        copy = pltpu.make_async_remote_copy(
            src_ref=source,
            dst_ref=outs[a].at[slot],
            send_sem=ring_send.at[a, way, step],
            recv_sem=ring_recv.at[a, way, step],
            device_id={"dp": (ahead, behind)[way]},
            device_id_type=pl.DeviceIdType.MESH,
        )
        copy.start()
        started.append(copy)
        return copy

    def share(a, source, slot, index):
        copy = pltpu.make_async_remote_copy(
            src_ref=source,
            dst_ref=outs[a].at[slot],
            send_sem=core_send.at[a, index],
            recv_sem=core_recv.at[a, index],
            device_id={"dp": partner},
            device_id_type=pl.DeviceIdType.MESH,
        )
        copy.start()
        if fused and a == 0:
            first[index] = copy
        else:
            across.append(copy)

    def compute(slot, block):
        size = block.shape[0]
        columns = pl.ds(pl.multiple_of(slot * size, BLOCK), size)
        tile = normed.shape[0] // 3

        def part(t, carry):
            at = pl.ds(pl.multiple_of(t * tile, tile), tile)
            before = lax.dot_general(
                normed[at, :],
                block[...],
                (((1,), (1,)), ((), ())),
                preferred_element_type=jnp.float32,
            )
            before = before + bias[slot]
            hidden[at, columns] = (
                0.5 * before * (1.0 + lax.erf(before * math.sqrt(0.5)))
            ).astype(hidden.dtype)
            return carry

        lax.fori_loop(0, 3, part, 0)

    first = {}

    def partner_block(index, step, way):
        first[index].wait_recv()
        slot = partner
        if index:
            slot = device(place + (1 + step) * turn * (1 - 2 * way)) + turn
        compute(slot, outs[0].at[slot])

    flying, local = {}, []
    for a in range(count):
        for way in range(2):
            flying[a, way] = send(a, ins[a], me, way, 0)
        share(a, ins[a], me, 0)
        if not (fused and a == 0):
            local.append(pltpu.make_async_copy(ins[a], outs[a].at[me], own_sem.at[a]))
            local[-1].start()
    if fused:
        compute(me, ins[0])
    for step in range(half):
        landed = []
        if fused:
            if step == 0:
                partner_block(0, 0, 0)
            for way in range(2):
                if 0 < step <= steps[way]:
                    partner_block(way * half + step, step - 1, way)
        for a in range(count):
            for way in range(2):
                if step >= steps[way]:
                    continue
                flying[a, way].wait_recv()
                slot = device(place - (1 + step) * turn * (1 - 2 * way))
                block = outs[a].at[slot]
                if step + 1 < steps[way]:
                    flying[a, way] = send(a, block, slot, way, step + 1)
                share(a, block, slot, 1 + way * half + step)
                if fused and a == 0:
                    landed.append((slot, block))
        for slot, block in landed:
            compute(slot, block)
    if fused:
        for way in range(2):
            if steps[way] == half:
                partner_block(way * half + half, half - 1, way)
        for copy in first.values():
            copy.wait_send()
    for copy in local:
        copy.wait()
    for copy in started:
        copy.wait_send()
    for copy in across:
        copy.wait()


def ring_gather(blocks, collective_id):
    devices = lax.axis_size("dp")
    chips, count = devices // 2, len(blocks)
    dma = pltpu.SemaphoreType.DMA
    return pl.pallas_call(
        functools.partial(ring_kernel, chips, count, False),
        out_shape=[jax.ShapeDtypeStruct((devices,) + b.shape, b.dtype) for b in blocks],
        in_specs=[pl.BlockSpec(memory_space=pl.ANY)] * count,
        out_specs=[pl.BlockSpec(memory_space=pl.ANY)] * count,
        scratch_shapes=[
            dma((count, 2, chips // 2)),
            dma((count, 2, chips // 2)),
            dma((count, chips)),
            dma((count, chips)),
            dma((count,)),
        ],
        compiler_params=pltpu.CompilerParams(collective_id=collective_id, has_side_effects=True),
    )(*blocks)


def ring_up(normed, bias, up, down, collective_id):
    devices = lax.axis_size("dp")
    chips = devices // 2
    dma = pltpu.SemaphoreType.DMA
    whole = pl.BlockSpec(memory_space=pltpu.VMEM)
    apart = pl.BlockSpec(memory_space=pl.ANY)
    return pl.pallas_call(
        functools.partial(ring_kernel, chips, 2, True),
        out_shape=[
            jax.ShapeDtypeStruct((normed.shape[0], devices * up.shape[0]), normed.dtype),
            jax.ShapeDtypeStruct((devices,) + down.shape, down.dtype),
        ],
        in_specs=[whole, whole, whole, apart],
        out_specs=[whole, apart],
        scratch_shapes=[
            pltpu.VMEM((devices,) + up.shape, up.dtype),
            dma((2, 2, chips // 2)),
            dma((2, 2, chips // 2)),
            dma((2, chips)),
            dma((2, chips)),
            dma((2,)),
        ],
        compiler_params=pltpu.CompilerParams(
            collective_id=collective_id, has_side_effects=True, vmem_limit_bytes=40 << 20
        ),
    )(normed, bias.reshape(devices, 1, -1), up, down)


def on_device(tokens, token_mask, span_ids, norm_gain, norm_shift, w_up, b_up, w_down):
    values = tokens.astype(jnp.float32)
    center = jnp.mean(values, axis=1, keepdims=True)
    spread = jnp.mean((values - center) ** 2, axis=1, keepdims=True)
    normed = ((values - center) * lax.rsqrt(spread + 1e-05) * norm_gain + norm_shift).astype(
        jnp.bfloat16
    )
    width, hidden_size = tokens.shape[1], b_up.shape[0]
    over_last = (((1,), (1,)), ((), ()))
    if w_up.shape[1] % BLOCK == 0:
        hidden, down_full = ring_up(normed, b_up, w_up.T, w_down.T, 0)
    else:
        up_full, down_full = ring_gather((w_up.T, w_down.T), 0)
        up_full = up_full.reshape(hidden_size, width)
        before = (
            lax.dot_general(normed, up_full, over_last, preferred_element_type=jnp.float32) + b_up
        )
        hidden = jax.nn.gelu(before, approximate=False).astype(jnp.bfloat16)
    down_full = down_full.reshape(width, hidden_size)
    projected = lax.dot_general(
        hidden, down_full, over_last, preferred_element_type=jnp.float32
    )
    block_out = (values + projected).astype(jnp.bfloat16)
    labels = jnp.arange(SEG_DEV, dtype=jnp.int32)[:, None]
    select = (span_ids[0][None, :] == labels) & (token_mask[0][None, :] == 1)
    sums = jnp.dot(select.astype(jnp.bfloat16), block_out, preferred_element_type=jnp.float32)
    counts = jnp.sum(select.astype(jnp.float32), axis=1)
    pooled = (sums / jnp.maximum(counts, 1.0)[:, None]).astype(jnp.bfloat16)
    (every,) = ring_gather((pooled,), 1)
    every = every.reshape(-1, width)
    gram = lax.dot_general(
        every, every, (((0,), (0,)), ((), ())), preferred_element_type=jnp.float32
    )
    total_rows = SEG_DEV * lax.axis_size("dp")
    return whiten(gram, pooled.astype(jnp.float32).T, math.sqrt(total_rows)).T


def solution(mesh):
    in_specs = (
        P(("groups", "dp"), None),
        P(("groups", "dp"), None),
        P(("groups", "dp"), None),
        P(),
        P(),
        P(None, "dp"),
        P(),
        P(None, "dp"),
    )
    out_specs = P(("groups", "dp"), None)
    return jax.shard_map(
        on_device, mesh=mesh, in_specs=in_specs, out_specs=out_specs, check_vma=False
    )
```

```python
import functools
import math

import jax
import jax.numpy as jnp
from jax import lax
from jax.experimental import pallas as pl
from jax.experimental.pallas import tpu as pltpu
from jax.sharding import PartitionSpec as P

SEG_DEV = 192
BLOCK = 128
HIGHEST = lax.Precision.HIGHEST


def inverse_factor(src, dst):
    lane = lax.broadcasted_iota(jnp.int32, (8, BLOCK), 1)
    sub = lax.broadcasted_iota(jnp.int32, (8, BLOCK), 0)
    groups = BLOCK // 8
    held = [src[8 * q : 8 * q + 8, :BLOCK] for q in range(groups)]

    def column(block, c):
        return jnp.broadcast_to(block[:, c : c + 1], (8, BLOCK))

    def row(block, r):
        return jnp.broadcast_to(block[r : r + 1, :], (8, BLOCK))

    for p in range(groups):
        at = 8 * p
        inside = (lane >= at) & (lane < at + 8)
        raw = held[p]
        cols = [column(raw, at + c) for c in range(8)]
        work = jnp.where(inside, jnp.where(lane - at == sub, 1.0, 0.0), raw)
        done = jnp.zeros((8, BLOCK), jnp.float32)
        for j in range(8):
            here = sub == j
            pivot = row(cols[j], j)
            inv = 1.0 / pivot
            done = jnp.where(here, work * lax.rsqrt(pivot), done)
            scaled = row(work, j) * inv
            work = jnp.where(here, scaled, work - cols[j] * scaled)
            for c in range(j + 1, 8):
                scaled = row(cols[c], j) * inv
                cols[c] = jnp.where(here, scaled, cols[c] - cols[j] * scaled)
        dst[at : at + 8, :] = jnp.where(lane <= at + sub, done, 0.0)
        rows = [row(work, c) for c in range(8)]
        for q in range(p + 1, groups):
            total = jnp.where(inside, 0.0, held[q])
            for c in range(8):
                total = total - column(held[q], at + c) * rows[c]
            held[q] = total


def whiten_kernel(scale, gram_ref, rows_ref, out_ref, a, panel, inv):
    n = gram_ref.shape[0]
    extra = rows_ref.shape[1]
    a[:, :n] = gram_ref[...]
    a[:, n:] = jnp.zeros((n, a.shape[1] - n), jnp.float32)
    a[:, n : n + extra] = rows_ref[...]
    blocks = n // BLOCK

    def step(k, carry):
        lo = pl.multiple_of(k * BLOCK, BLOCK)
        panel[:, :BLOCK] = a[pl.ds(lo, BLOCK), pl.ds(lo, BLOCK)]
        inverse_factor(panel, inv)
        panel[...] = jnp.dot(
            inv[...], a[pl.ds(lo, BLOCK), :], preferred_element_type=jnp.float32, precision=HIGHEST
        )
        out_ref[pl.ds(lo, BLOCK), :] = panel[:, n : n + extra] * scale

        for first in range(0, blocks, 2):
            start = first * BLOCK

            def trail(i, carry, start=start):
                hi = pl.multiple_of(i * BLOCK, BLOCK)
                left = panel[:, pl.ds(hi, BLOCK)].T
                a[pl.ds(hi, BLOCK), start:] -= jnp.dot(
                    left, panel[:, start:], preferred_element_type=jnp.float32, precision=HIGHEST
                )
                return carry

            lax.fori_loop(jnp.maximum(k + 1, first), min(first + 2, blocks), trail, 0)
        return carry

    lax.fori_loop(0, blocks, step, 0)


def whiten(gram, rows_t, scale):
    n, extra = rows_t.shape
    wide = n + (extra + BLOCK - 1) // BLOCK * BLOCK
    return pl.pallas_call(
        functools.partial(whiten_kernel, scale),
        out_shape=jax.ShapeDtypeStruct((n, extra), jnp.float32),
        in_specs=[pl.BlockSpec(memory_space=pltpu.VMEM)] * 2,
        out_specs=pl.BlockSpec(memory_space=pltpu.VMEM),
        scratch_shapes=[
            pltpu.VMEM((n, wide), jnp.float32),
            pltpu.VMEM((BLOCK, wide), jnp.float32),
            pltpu.VMEM((BLOCK, BLOCK), jnp.float32),
        ],
        compiler_params=pltpu.CompilerParams(vmem_limit_bytes=32 << 20),
    )(gram, rows_t)


def ring_kernel(chips, count, fused, *refs):
    if fused:
        normed, bias, up, down, hidden, down_out, up_out = refs[:7]
        ins, outs, refs = (up, down), (up_out, down_out), refs[7:]
    else:
        ins, outs, refs = refs[:count], refs[count : 2 * count], refs[2 * count :]
    ring_send, ring_recv, core_send, core_recv, own_sem = refs
    me = lax.axis_index("dp")
    core, chip = lax.rem(me, 2), me // 2
    half = chips // 2
    odd = lax.rem(chip, 2)
    place = (1 - odd) * (chip // 2) + odd * (chips - 1 - chip // 2)
    turn = 1 - 2 * core
    partner = me + turn

    def device(q):
        q = lax.rem(q + 2 * chips, chips)
        back = q // half
        return 2 * ((1 - back) * 2 * q + back * (2 * (chips - 1 - q) + 1)) + core

    ahead, behind = device(place + turn), device(place - turn)
    barrier = pltpu.get_barrier_semaphore()
    for other in (ahead, behind, partner):
        pl.semaphore_signal(
            barrier, inc=1, device_id={"dp": other}, device_id_type=pl.DeviceIdType.MESH
        )
    pl.semaphore_wait(barrier, 3)

    steps = (half, chips - 1 - half)
    started, across = [], []

    def send(a, source, slot, way, step):
        copy = pltpu.make_async_remote_copy(
            src_ref=source,
            dst_ref=outs[a].at[slot],
            send_sem=ring_send.at[a, way, step],
            recv_sem=ring_recv.at[a, way, step],
            device_id={"dp": (ahead, behind)[way]},
            device_id_type=pl.DeviceIdType.MESH,
        )
        copy.start()
        started.append(copy)
        return copy

    def share(a, source, slot, index):
        copy = pltpu.make_async_remote_copy(
            src_ref=source,
            dst_ref=outs[a].at[slot],
            send_sem=core_send.at[a, index],
            recv_sem=core_recv.at[a, index],
            device_id={"dp": partner},
            device_id_type=pl.DeviceIdType.MESH,
        )
        copy.start()
        if fused and a == 0:
            first[index] = copy
        else:
            across.append(copy)

    def compute(slot, block):
        size = block.shape[0]
        columns = pl.ds(pl.multiple_of(slot * size, BLOCK), size)
        tile = normed.shape[0] // 3

        def part(t, carry):
            at = pl.ds(pl.multiple_of(t * tile, tile), tile)
            before = lax.dot_general(
                normed[at, :],
                block[...],
                (((1,), (1,)), ((), ())),
                preferred_element_type=jnp.float32,
            )
            before = before + bias[slot]
            hidden[at, columns] = (
                0.5 * before * (1.0 + lax.erf(before * math.sqrt(0.5)))
            ).astype(hidden.dtype)
            return carry

        lax.fori_loop(0, 3, part, 0)

    first = {}

    def partner_block(index, step, way):
        first[index].wait_recv()
        slot = partner
        if index:
            slot = device(place + (1 + step) * turn * (1 - 2 * way)) + turn
        compute(slot, outs[0].at[slot])

    flying, local = {}, []
    for a in range(count):
        for way in range(2):
            flying[a, way] = send(a, ins[a], me, way, 0)
        share(a, ins[a], me, 0)
        if not (fused and a == 0):
            local.append(pltpu.make_async_copy(ins[a], outs[a].at[me], own_sem.at[a]))
            local[-1].start()
    if fused:
        compute(me, ins[0])
    for step in range(half):
        landed = []
        if fused:
            if step == 0:
                partner_block(0, 0, 0)
            for way in range(2):
                if 0 < step <= steps[way]:
                    partner_block(way * half + step, step - 1, way)
        for a in range(count):
            for way in range(2):
                if step >= steps[way]:
                    continue
                flying[a, way].wait_recv()
                slot = device(place - (1 + step) * turn * (1 - 2 * way))
                block = outs[a].at[slot]
                if step + 1 < steps[way]:
                    flying[a, way] = send(a, block, slot, way, step + 1)
                share(a, block, slot, 1 + way * half + step)
                if fused and a == 0:
                    landed.append((slot, block))
        for slot, block in landed:
            compute(slot, block)
    if fused:
        for way in range(2):
            if steps[way] == half:
                partner_block(way * half + half, half - 1, way)
        for copy in first.values():
            copy.wait_send()
    for copy in local:
        copy.wait()
    for copy in started:
        copy.wait_send()
    for copy in across:
        copy.wait()


def ring_gather(blocks, collective_id):
    devices = lax.axis_size("dp")
    chips, count = devices // 2, len(blocks)
    dma = pltpu.SemaphoreType.DMA
    return pl.pallas_call(
        functools.partial(ring_kernel, chips, count, False),
        out_shape=[jax.ShapeDtypeStruct((devices,) + b.shape, b.dtype) for b in blocks],
        in_specs=[pl.BlockSpec(memory_space=pl.ANY)] * count,
        out_specs=[pl.BlockSpec(memory_space=pl.ANY)] * count,
        scratch_shapes=[
            dma((count, 2, chips // 2)),
            dma((count, 2, chips // 2)),
            dma((count, chips)),
            dma((count, chips)),
            dma((count,)),
        ],
        compiler_params=pltpu.CompilerParams(collective_id=collective_id, has_side_effects=True),
    )(*blocks)


def ring_up(normed, bias, up, down, collective_id):
    devices = lax.axis_size("dp")
    chips = devices // 2
    dma = pltpu.SemaphoreType.DMA
    whole = pl.BlockSpec(memory_space=pltpu.VMEM)
    apart = pl.BlockSpec(memory_space=pl.ANY)
    return pl.pallas_call(
        functools.partial(ring_kernel, chips, 2, True),
        out_shape=[
            jax.ShapeDtypeStruct((normed.shape[0], devices * up.shape[0]), normed.dtype),
            jax.ShapeDtypeStruct((devices,) + down.shape, down.dtype),
        ],
        in_specs=[whole, whole, whole, apart],
        out_specs=[whole, apart],
        scratch_shapes=[
            pltpu.VMEM((devices,) + up.shape, up.dtype),
            dma((2, 2, chips // 2)),
            dma((2, 2, chips // 2)),
            dma((2, chips)),
            dma((2, chips)),
            dma((2,)),
        ],
        compiler_params=pltpu.CompilerParams(
            collective_id=collective_id, has_side_effects=True, vmem_limit_bytes=40 << 20
        ),
    )(normed, bias.reshape(devices, 1, -1), up, down)


def on_device(tokens, token_mask, span_ids, norm_gain, norm_shift, w_up, b_up, w_down):
    values = tokens.astype(jnp.float32)
    center = jnp.mean(values, axis=1, keepdims=True)
    spread = jnp.mean((values - center) ** 2, axis=1, keepdims=True)
    normed = ((values - center) * lax.rsqrt(spread + 1e-05) * norm_gain + norm_shift).astype(
        jnp.bfloat16
    )
    width, hidden_size = tokens.shape[1], b_up.shape[0]
    over_last = (((1,), (1,)), ((), ()))
    if w_up.shape[1] % BLOCK == 0:
        hidden, down_full = ring_up(normed, b_up, w_up.T, w_down.T, 0)
    else:
        up_full, down_full = ring_gather((w_up.T, w_down.T), 0)
        up_full = up_full.reshape(hidden_size, width)
        before = (
            lax.dot_general(normed, up_full, over_last, preferred_element_type=jnp.float32) + b_up
        )
        hidden = jax.nn.gelu(before, approximate=False).astype(jnp.bfloat16)
    down_full = down_full.reshape(width, hidden_size)
    projected = lax.dot_general(
        hidden, down_full, over_last, preferred_element_type=jnp.float32
    )
    block_out = (values + projected).astype(jnp.bfloat16)
    labels = jnp.arange(SEG_DEV, dtype=jnp.int32)[:, None]
    select = (span_ids[0][None, :] == labels) & (token_mask[0][None, :] == 1)
    sums = jnp.dot(select.astype(jnp.bfloat16), block_out, preferred_element_type=jnp.float32)
    counts = jnp.sum(select.astype(jnp.float32), axis=1)
    pooled = (sums / jnp.maximum(counts, 1.0)[:, None]).astype(jnp.bfloat16)
    (every,) = ring_gather((pooled,), 1)
    every = every.reshape(-1, width)
    gram = lax.dot_general(
        every, every, (((0,), (0,)), ((), ())), preferred_element_type=jnp.float32
    )
    total_rows = SEG_DEV * lax.axis_size("dp")
    return whiten(gram, pooled.astype(jnp.float32).T, math.sqrt(total_rows)).T


def solution(mesh):
    in_specs = (
        P(("groups", "dp"), None),
        P(("groups", "dp"), None),
        P(("groups", "dp"), None),
        P(),
        P(),
        P(None, "dp"),
        P(),
        P(None, "dp"),
    )
    out_specs = P(("groups", "dp"), None)
    return jax.shard_map(
        on_device, mesh=mesh, in_specs=in_specs, out_specs=out_specs, check_vma=False
    )
```

```python
import functools
import math

import jax
import jax.numpy as jnp
from jax import lax
from jax.experimental import pallas as pl
from jax.experimental.pallas import tpu as pltpu
from jax.sharding import PartitionSpec as P

SEG_DEV = 192
BLOCK = 128
HIGHEST = lax.Precision.HIGHEST


def inverse_factor(src, dst):
    lane = lax.broadcasted_iota(jnp.int32, (8, BLOCK), 1)
    sub = lax.broadcasted_iota(jnp.int32, (8, BLOCK), 0)
    groups = BLOCK // 8
    held = [src[8 * q : 8 * q + 8, :BLOCK] for q in range(groups)]

    def column(block, c):
        return jnp.broadcast_to(block[:, c : c + 1], (8, BLOCK))

    def row(block, r):
        return jnp.broadcast_to(block[r : r + 1, :], (8, BLOCK))

    for p in range(groups):
        at = 8 * p
        inside = (lane >= at) & (lane < at + 8)
        raw = held[p]
        cols = [column(raw, at + c) for c in range(8)]
        work = jnp.where(inside, jnp.where(lane - at == sub, 1.0, 0.0), raw)
        done = jnp.zeros((8, BLOCK), jnp.float32)
        for j in range(8):
            here = sub == j
            pivot = row(cols[j], j)
            inv = 1.0 / pivot
            done = jnp.where(here, work * lax.rsqrt(pivot), done)
            scaled = row(work, j) * inv
            work = jnp.where(here, scaled, work - cols[j] * scaled)
            for c in range(j + 1, 8):
                scaled = row(cols[c], j) * inv
                cols[c] = jnp.where(here, scaled, cols[c] - cols[j] * scaled)
        dst[at : at + 8, :] = jnp.where(lane <= at + sub, done, 0.0)
        rows = [row(work, c) for c in range(8)]
        for q in range(p + 1, groups):
            total = jnp.where(inside, 0.0, held[q])
            for c in range(8):
                total = total - column(held[q], at + c) * rows[c]
            held[q] = total


def whiten_kernel(scale, first_ref, cross_ref, last_ref, rows_ref, out_ref, a, panel, inv):
    half = first_ref.shape[0]
    n = 2 * half
    extra = rows_ref.shape[1]
    a[:half, :half] = first_ref[...]
    a[:half, half:n] = cross_ref[...]
    a[half:, :half] = jnp.zeros((half, half), jnp.float32)
    a[half:, half:n] = last_ref[...]
    a[:, n:] = jnp.zeros((n, a.shape[1] - n), jnp.float32)
    a[:, n : n + extra] = rows_ref[...]
    blocks = n // BLOCK

    def step(k, carry):
        lo = pl.multiple_of(k * BLOCK, BLOCK)
        panel[:, :BLOCK] = a[pl.ds(lo, BLOCK), pl.ds(lo, BLOCK)]
        inverse_factor(panel, inv)
        panel[...] = jnp.dot(
            inv[...], a[pl.ds(lo, BLOCK), :], preferred_element_type=jnp.float32, precision=HIGHEST
        )
        out_ref[pl.ds(lo, BLOCK), :] = panel[:, n : n + extra] * scale

        for first in range(0, blocks, 2):
            start = first * BLOCK

            def trail(i, carry, start=start):
                hi = pl.multiple_of(i * BLOCK, BLOCK)
                left = panel[:, pl.ds(hi, BLOCK)].T
                a[pl.ds(hi, BLOCK), start:] -= jnp.dot(
                    left, panel[:, start:], preferred_element_type=jnp.float32, precision=HIGHEST
                )
                return carry

            lax.fori_loop(jnp.maximum(k + 1, first), min(first + 2, blocks), trail, 0)
        return carry

    lax.fori_loop(0, blocks, step, 0)


def whiten(gram, rows_t, scale):
    n, extra = rows_t.shape
    wide = n + (extra + BLOCK - 1) // BLOCK * BLOCK
    return pl.pallas_call(
        functools.partial(whiten_kernel, scale),
        out_shape=jax.ShapeDtypeStruct((n, extra), jnp.float32),
        in_specs=[pl.BlockSpec(memory_space=pltpu.VMEM)] * 4,
        out_specs=pl.BlockSpec(memory_space=pltpu.VMEM),
        scratch_shapes=[
            pltpu.VMEM((n, wide), jnp.float32),
            pltpu.VMEM((BLOCK, wide), jnp.float32),
            pltpu.VMEM((BLOCK, BLOCK), jnp.float32),
        ],
        compiler_params=pltpu.CompilerParams(vmem_limit_bytes=32 << 20),
    )(*gram, rows_t)


def ring_kernel(chips, count, fused, *refs):
    if fused:
        normed, bias, up, down, hidden, down_out, up_out = refs[:7]
        ins, outs, refs = (up, down), (up_out, down_out), refs[7:]
    else:
        ins, outs, refs = refs[:count], refs[count : 2 * count], refs[2 * count :]
    ring_send, ring_recv, core_send, core_recv, own_sem = refs
    me = lax.axis_index("dp")
    core, chip = lax.rem(me, 2), me // 2
    half = chips // 2
    odd = lax.rem(chip, 2)
    place = (1 - odd) * (chip // 2) + odd * (chips - 1 - chip // 2)
    turn = 1 - 2 * core
    partner = me + turn

    def device(q):
        q = lax.rem(q + 2 * chips, chips)
        back = q // half
        return 2 * ((1 - back) * 2 * q + back * (2 * (chips - 1 - q) + 1)) + core

    ahead, behind = device(place + turn), device(place - turn)
    barrier = pltpu.get_barrier_semaphore()
    for other in (ahead, behind, partner):
        pl.semaphore_signal(
            barrier, inc=1, device_id={"dp": other}, device_id_type=pl.DeviceIdType.MESH
        )
    pl.semaphore_wait(barrier, 3)

    steps = (half, chips - 1 - half)
    started, across = [], []

    def send(a, source, slot, way, step):
        copy = pltpu.make_async_remote_copy(
            src_ref=source,
            dst_ref=outs[a].at[slot],
            send_sem=ring_send.at[a, way, step],
            recv_sem=ring_recv.at[a, way, step],
            device_id={"dp": (ahead, behind)[way]},
            device_id_type=pl.DeviceIdType.MESH,
        )
        copy.start()
        started.append(copy)
        return copy

    def share(a, source, slot, index):
        copy = pltpu.make_async_remote_copy(
            src_ref=source,
            dst_ref=outs[a].at[slot],
            send_sem=core_send.at[a, index],
            recv_sem=core_recv.at[a, index],
            device_id={"dp": partner},
            device_id_type=pl.DeviceIdType.MESH,
        )
        copy.start()
        if fused and a == 0:
            first[index] = copy
        else:
            across.append(copy)

    def compute(slot, block):
        size = block.shape[0]
        columns = pl.ds(pl.multiple_of(slot * size, BLOCK), size)
        tile = normed.shape[0] // 3

        def part(t, carry):
            at = pl.ds(pl.multiple_of(t * tile, tile), tile)
            before = lax.dot_general(
                normed[at, :],
                block[...],
                (((1,), (1,)), ((), ())),
                preferred_element_type=jnp.float32,
            )
            before = before + bias[slot]
            hidden[at, columns] = (
                0.5 * before * (1.0 + lax.erf(before * math.sqrt(0.5)))
            ).astype(hidden.dtype)
            return carry

        lax.fori_loop(0, 3, part, 0)

    first = {}

    def partner_block(index, step, way):
        first[index].wait_recv()
        slot = partner
        if index:
            slot = device(place + (1 + step) * turn * (1 - 2 * way)) + turn
        compute(slot, outs[0].at[slot])

    flying, local = {}, []
    for a in range(count):
        for way in range(2):
            flying[a, way] = send(a, ins[a], me, way, 0)
        share(a, ins[a], me, 0)
        if not (fused and a == 0):
            local.append(pltpu.make_async_copy(ins[a], outs[a].at[me], own_sem.at[a]))
            local[-1].start()
    if fused:
        compute(me, ins[0])
    for step in range(half):
        landed = []
        if fused:
            if step == 0:
                partner_block(0, 0, 0)
            for way in range(2):
                if 0 < step <= steps[way]:
                    partner_block(way * half + step, step - 1, way)
        for a in range(count):
            for way in range(2):
                if step >= steps[way]:
                    continue
                flying[a, way].wait_recv()
                slot = device(place - (1 + step) * turn * (1 - 2 * way))
                block = outs[a].at[slot]
                if step + 1 < steps[way]:
                    flying[a, way] = send(a, block, slot, way, step + 1)
                share(a, block, slot, 1 + way * half + step)
                if fused and a == 0:
                    landed.append((slot, block))
        for slot, block in landed:
            compute(slot, block)
    if fused:
        for way in range(2):
            if steps[way] == half:
                partner_block(way * half + half, half - 1, way)
        for copy in first.values():
            copy.wait_send()
    for copy in local:
        copy.wait()
    for copy in started:
        copy.wait_send()
    for copy in across:
        copy.wait()


def ring_gather(blocks, collective_id):
    devices = lax.axis_size("dp")
    chips, count = devices // 2, len(blocks)
    dma = pltpu.SemaphoreType.DMA
    return pl.pallas_call(
        functools.partial(ring_kernel, chips, count, False),
        out_shape=[jax.ShapeDtypeStruct((devices,) + b.shape, b.dtype) for b in blocks],
        in_specs=[pl.BlockSpec(memory_space=pl.ANY)] * count,
        out_specs=[pl.BlockSpec(memory_space=pl.ANY)] * count,
        scratch_shapes=[
            dma((count, 2, chips // 2)),
            dma((count, 2, chips // 2)),
            dma((count, chips)),
            dma((count, chips)),
            dma((count,)),
        ],
        compiler_params=pltpu.CompilerParams(collective_id=collective_id, has_side_effects=True),
    )(*blocks)


def ring_up(normed, bias, up, down, collective_id):
    devices = lax.axis_size("dp")
    chips = devices // 2
    dma = pltpu.SemaphoreType.DMA
    whole = pl.BlockSpec(memory_space=pltpu.VMEM)
    apart = pl.BlockSpec(memory_space=pl.ANY)
    return pl.pallas_call(
        functools.partial(ring_kernel, chips, 2, True),
        out_shape=[
            jax.ShapeDtypeStruct((normed.shape[0], devices * up.shape[0]), normed.dtype),
            jax.ShapeDtypeStruct((devices,) + down.shape, down.dtype),
        ],
        in_specs=[whole, whole, whole, apart],
        out_specs=[whole, apart],
        scratch_shapes=[
            pltpu.VMEM((devices,) + up.shape, up.dtype),
            dma((2, 2, chips // 2)),
            dma((2, 2, chips // 2)),
            dma((2, chips)),
            dma((2, chips)),
            dma((2,)),
        ],
        compiler_params=pltpu.CompilerParams(
            collective_id=collective_id, has_side_effects=True, vmem_limit_bytes=40 << 20
        ),
    )(normed, bias.reshape(devices, 1, -1), up, down)


def on_device(tokens, token_mask, span_ids, norm_gain, norm_shift, w_up, b_up, w_down):
    values = tokens.astype(jnp.float32)
    center = jnp.mean(values, axis=1, keepdims=True)
    spread = jnp.mean((values - center) ** 2, axis=1, keepdims=True)
    normed = ((values - center) * lax.rsqrt(spread + 1e-05) * norm_gain + norm_shift).astype(
        jnp.bfloat16
    )
    width, hidden_size = tokens.shape[1], b_up.shape[0]
    over_last = (((1,), (1,)), ((), ()))
    if w_up.shape[1] % BLOCK == 0:
        hidden, down_full = ring_up(normed, b_up, w_up.T, w_down.T, 0)
    else:
        up_full, down_full = ring_gather((w_up.T, w_down.T), 0)
        up_full = up_full.reshape(hidden_size, width)
        before = (
            lax.dot_general(normed, up_full, over_last, preferred_element_type=jnp.float32) + b_up
        )
        hidden = jax.nn.gelu(before, approximate=False).astype(jnp.bfloat16)
    down_full = down_full.reshape(width, hidden_size)
    projected = lax.dot_general(
        hidden, down_full, over_last, preferred_element_type=jnp.float32
    )
    block_out = (values + projected).astype(jnp.bfloat16)
    labels = jnp.arange(SEG_DEV, dtype=jnp.int32)[:, None]
    select = (span_ids[0][None, :] == labels) & (token_mask[0][None, :] == 1)
    sums = jnp.dot(select.astype(jnp.bfloat16), block_out, preferred_element_type=jnp.float32)
    counts = jnp.sum(select.astype(jnp.float32), axis=1)
    pooled = (sums / jnp.maximum(counts, 1.0)[:, None]).astype(jnp.bfloat16)
    middle = width // 2
    left, right = (
        half.reshape(-1, middle)
        for half in ring_gather((pooled[:, :middle], pooled[:, middle:]), 1)
    )
    gram = [
        lax.dot_general(one, two, (((0,), (0,)), ((), ())), preferred_element_type=jnp.float32)
        for one, two in ((left, left), (left, right), (right, right))
    ]
    total_rows = SEG_DEV * lax.axis_size("dp")
    return whiten(gram, pooled.astype(jnp.float32).T, math.sqrt(total_rows)).T


def solution(mesh):
    in_specs = (
        P(("groups", "dp"), None),
        P(("groups", "dp"), None),
        P(("groups", "dp"), None),
        P(),
        P(),
        P(None, "dp"),
        P(),
        P(None, "dp"),
    )
    out_specs = P(("groups", "dp"), None)
    return jax.shard_map(
        on_device, mesh=mesh, in_specs=in_specs, out_specs=out_specs, check_vma=False
    )
```
